32 devices in a mesh: fsdp: 4 (over z), replica: 2 (over x), tensor: 4 (over y, core).
Axes of the slice: x: 2, y: 2, z: 4, core: 2. Of those that a mesh axis runs over, the one named last changes fastest.
Arguments:
- tokens: bfloat16 [1024, 8192], P(('fsdp', 'replica')), may hold values from -6 to 6
- weight_codes: bfloat16 [8192, 14336], P('fsdp', 'tensor'), may hold values from -127 to 127, as said below
- scales: float32 [64, 14336], P('fsdp', 'tensor'), may hold values from 3e-05 to 0.0003
- cotangent: bfloat16 [1024, 14336], P(('fsdp', 'replica'), 'tensor'), may hold values from -6 to 6
- sign_bits: int32 [14336], P('tensor'), may hold values from 0 to 1
Outputs:
- activation: bfloat16 [1024, 14336], P(('fsdp', 'replica'), 'tensor')
- input_grad: bfloat16 [1024, 8192], P(('fsdp', 'replica'), 'tensor')
- grad_codes: float32 [8192, 14336], P(('fsdp', 'replica'), 'tensor')
The draws below stay inside these ranges and needn't reach their ends.
Inputs may be any that keep to these rules, and one draw needn't show every extreme that they name: `weight_codes`: integer values, held exactly.
All inputs are finite; a program needn't handle non-finite values.
Results may differ from the reference program's by a relative error of at most 0.015.
Values may be sent and summed in bfloat16 or wider, within the bound.
A program may use at most 128 MiB of HBM per device.

```python
import math
import jax
import jax.numpy as jnp
from jax import lax

D = 8192
FF = 14336
QB = 128
HB = 128
TOKENS = 1024
N_FSDP = 4
N_TENSOR = 4


def draw_weight_codes(key, part):
    return jax.random.randint(key, (D, FF), -127, 128).astype(jnp.float32).astype(jnp.bfloat16)


def plant(result, stream_key, least, top_value):
    longest = result.shape.index(max(result.shape))
    spots = []
    for shift in (0, 1):
        where = [jax.random.randint(jax.random.fold_in(stream_key, axis), (), 0, length) for axis, length in enumerate(result.shape)]
        where[longest] = (where[longest] + shift) % result.shape[longest]
        spots.append(tuple(where))
    return result.at[spots[0]].set(least).at[spots[1]].set(top_value)


def block_levels(own_key, dims, shards, low, top_value):
    def one(dim, shards_of):
        heights = jax.random.uniform(jax.random.fold_in(jax.random.fold_in(own_key, 6), dim), (shards_of,), jnp.float32, low / len(shards), top_value / len(shards))
        return jnp.repeat(jnp.exp(heights), dims[dim] // shards_of).reshape((-1,) + (1,) * (len(dims) - dim - 1))

    level = one(*shards[0])
    for cut in shards[1:]:
        level = level * one(*cut)
    return level


def scatter_about(key, dims, scale, limit, split=(), kind=jnp.bfloat16):
    values = jax.random.normal(key, dims, jnp.float32) * scale
    if len(split) > 0:
        values = block_levels(key, dims, split, -0.22, 0.18) * values
    return jnp.clip(values, min=-limit, max=limit).astype(kind)


def setup_inputs(seed: int = 0) -> dict:
    arg_keys = jax.random.split(jax.random.key(seed), 6)
    return {
        "tokens": scatter_about(arg_keys[0], (TOKENS, D), 1.0, 6.0, ((0, 8),)),
        "weight_codes": draw_weight_codes(jax.random.fold_in(arg_keys[5], 71), 0),
        "scales": jnp.clip(jnp.exp(math.log(0.0003) - 2.3025852 * jax.random.uniform(arg_keys[2], (D // QB, FF), jnp.float32) ** block_levels(arg_keys[2], (D // QB, FF), ((0, 4), (1, 4)), -0.2, 0.2)), 2.9999999242136255e-05, 0.0003),
        "cotangent": scatter_about(arg_keys[3], (TOKENS, FF), 1.0, 6.0, ((0, 8), (1, 4))),
        "sign_bits": plant(jax.random.randint(arg_keys[4], (FF,), 0, 2), jax.random.fold_in(arg_keys[4], 1), 0, 1).astype(jnp.int32),
    }


def hadamard_table(length):
    indices = jnp.arange(length, dtype=jnp.int32)
    intersection_bits = jnp.bitwise_and(indices[:, None], indices[None, :])
    parity = jnp.zeros((length, length), jnp.int32)
    for bit_pos in range(length.bit_length() - 1):
        parity = parity + jnp.bitwise_and(jnp.right_shift(intersection_bits, bit_pos), 1)
    return (1 - 2 * (parity % 2)).astype(jnp.float32)

def rotate_blocks(matrix, sign_bits, scaling):
    height, width = matrix.shape
    signed = matrix * (2 * sign_bits - 1).astype(jnp.float32)[None, :]
    blocks = signed.reshape(height, width // HB, HB)
    turned = jnp.einsum('rbi,ij->rbj', blocks, hadamard_table(HB), precision=lax.Precision.HIGHEST)
    return turned.reshape(height, width) * scaling

def reference(tokens, weight_codes, scales, cotangent, sign_bits):
    weight = (weight_codes.astype(jnp.float32).reshape(D // QB, QB, FF) * scales[:, None, :]).reshape(D, FF).astype(jnp.bfloat16)
    shard_rows = D // N_FSDP

    def add_shard(totals, position):
        offset = (position * shard_rows).astype(jnp.int32)
        token_part = lax.dynamic_slice_in_dim(tokens, offset, shard_rows, 1)
        weight_part = lax.dynamic_slice_in_dim(weight, offset, shard_rows, 0)
        product = jnp.dot(token_part, weight_part, preferred_element_type=jnp.float32).astype(jnp.bfloat16)
        product = lax.optimization_barrier(product)
        return (totals + product.astype(jnp.float32), None)
    hidden, _ = lax.scan(add_shard, jnp.zeros((TOKENS, FF), jnp.float32), jnp.arange(N_FSDP, dtype=jnp.int32))
    sigmoid_val = jax.nn.sigmoid(hidden)
    activation = (hidden * sigmoid_val).astype(jnp.bfloat16)
    hidden_grad = (cotangent.astype(jnp.float32) * sigmoid_val * (1.0 + hidden * (1.0 - sigmoid_val))).astype(jnp.bfloat16)
    weight_grad = jnp.dot(tokens.T, hidden_grad, preferred_element_type=jnp.float32)
    scaling = 1.0 / jnp.sqrt(jnp.float32(HB) * jnp.float32(TOKENS))
    grad_codes = rotate_blocks(weight_grad, sign_bits, scaling)
    quarter = FF // N_TENSOR

    def add_quarter(totals, position):
        offset = (position * quarter).astype(jnp.int32)
        grad_part = lax.dynamic_slice_in_dim(hidden_grad, offset, quarter, 1)
        weight_part = lax.dynamic_slice_in_dim(weight, offset, quarter, 1)
        product = jnp.dot(grad_part, weight_part.T, preferred_element_type=jnp.float32).astype(jnp.bfloat16)
        product = lax.optimization_barrier(product)
        return (totals + product.astype(jnp.float32), None)
    summed, _ = lax.scan(add_quarter, jnp.zeros((TOKENS, D), jnp.float32), jnp.arange(N_TENSOR, dtype=jnp.int32))
    return (activation, summed.astype(jnp.bfloat16), grad_codes)
```

```python
import functools

import jax
import jax.numpy as jnp
from jax import lax
from jax.experimental import pallas as pl
from jax.experimental.pallas import tpu as pltpu
from jax.sharding import PartitionSpec as P

HB = 128


def hadamard_table(length):
    indices = jnp.arange(length, dtype=jnp.int32)
    intersection_bits = jnp.bitwise_and(indices[:, None], indices[None, :])
    parity = jnp.zeros((length, length), jnp.int32)
    for bit_pos in range(length.bit_length() - 1):
        parity = parity + jnp.bitwise_and(jnp.right_shift(intersection_bits, bit_pos), 1)
    return (1 - 2 * (parity % 2)).astype(jnp.bfloat16)


def grad_kernel(scaling, turned_ref, mine_ref, other_ref, sign_ref, table_ref, out_ref, rotated):
    half, width = mine_ref.shape
    for part, ref in enumerate((mine_ref, other_ref)):
        for block in range(width // HB):
            cols = slice(block * HB, (block + 1) * HB)
            signed = ref[:, cols] * sign_ref[:, cols]
            rotated[part * half:(part + 1) * half, cols] = jnp.dot(
                signed, table_ref[...], preferred_element_type=jnp.float32
            ).astype(jnp.bfloat16)
    out_ref[...] = scaling * jnp.dot(turned_ref[...], rotated[...], preferred_element_type=jnp.float32)


def rotated_grad(turned, mine, other, sign_bits):
    rows, total = turned.shape
    half, width = mine.shape
    tile = next(t for t in (512, 256, HB) if width % t == 0)
    signs = (2 * sign_bits - 1).astype(jnp.bfloat16)[None, :]
    scaling = float(1.0 / (HB * total) ** 0.5)
    column = lambda c: (0, c)
    fixed = lambda c: (0, 0)
    return pl.pallas_call(
        functools.partial(grad_kernel, scaling),
        grid=(width // tile,),
        out_shape=jax.ShapeDtypeStruct((rows, width), jnp.float32),
        in_specs=[
            pl.BlockSpec((rows, total), fixed),
            pl.BlockSpec((half, tile), column),
            pl.BlockSpec((half, tile), column),
            pl.BlockSpec((1, tile), column),
            pl.BlockSpec((HB, HB), fixed),
        ],
        out_specs=pl.BlockSpec((rows, tile), column),
        scratch_shapes=[pltpu.VMEM((total, tile), jnp.bfloat16)],
        compiler_params=pltpu.CompilerParams(vmem_limit_bytes=48 * 1024 * 1024),
        cost_estimate=pl.CostEstimate(
            flops=2 * rows * total * width, bytes_accessed=4 * rows * width + 2 * total * width, transcendentals=0
        ),
        name="rotated_grad",
    )(turned, mine, other, signs, hadamard_table(HB))


MESH = pl.DeviceIdType.MESH
LAG = 2


def rotation_table(length):
    table = hadamard_table(HB)
    empty = jnp.zeros_like(table)
    count = length // HB
    return jnp.concatenate(
        [jnp.concatenate([table if i == j else empty for j in range(count)], 1) for i in range(count)], 0
    )


def exchange_kernel(
    n, parts, width, quant, span,
    tokens_hbm, codes_hbm, scales_hbm, cot_hbm, sign_ref, table_ref,
    act_hbm, turned_hbm, rotated_hbm, grad_hbm, last_ref,
    columns, across, turned, weight, scales, cot, act, part, from_left, from_right, mine, other,
    stage, product, total, whole, pair_in, pair_sum, over_in, quarter, landing, grad, pair_last, sum_last, over_last,
    load_sem, fetched, own_sem, act_sem, turned_sem, stage_sem, grad_sem,
    out_sent, out_came, mate_sent, mate_came, over_sent, over_came, relay_sent, relay_came,
    swap_sem, sum_sent, left_came, right_came, up_sent, down_sent, came, cross_sent, cross_came,
    pair_sem, flip_sem, line_sent, line_came, deal_sent, deal_came,
):
    me, t, r = lax.axis_index("fsdp"), lax.axis_index("tensor"), lax.axis_index("replica")
    lane, row = t % 2, t // 2
    mate, over, cross_over, twin = t + 1 - 2 * lane, (t + 2) % 4, 3 - t, 1 - r
    high, low = jnp.minimum(me + 1, n - 1), jnp.maximum(me - 1, 0)
    has_low, has_high = me > 0, me < n - 1
    depth = tokens_hbm.shape[1] // n
    rows = tokens_hbm.shape[0] // parts
    piece, eighth, half = depth // 4, depth // 8, depth // 2
    chunks = weight.shape[0]
    items = parts * chunks
    held = n * rows

    def ds(index, size):
        return pl.ds(pl.multiple_of(index * size, size), size)

    def remote(src, dst, sent, arrival, **device):
        return pltpu.make_async_remote_copy(
            src_ref=src, dst_ref=dst, send_sem=sent, recv_sem=arrival, device_id=device, device_id_type=MESH
        )

    def each(act_on):
        for k in range(1, n):
            for s in (me - k, me + k):
                @pl.when(jnp.logical_and(s >= 0, s < n))
                def _():
                    act_on(s)

    def others(index, count, act_on):
        for k in range(count):
            @pl.when(index != k)
            def _():
                act_on(k)

    def spot(p, s, q):
        return columns.at[p, ds(s, rows), ds(q, piece)]

    def send_out(p, f):
        return remote(
            tokens_hbm.at[ds(p, rows), ds(f * 4 + t, piece)], spot(p, me, t),
            out_sent.at[p, f], out_came.at[p, me], fsdp=f,
        )

    def receive_out(p, s):
        return remote(spot(p, s, t), spot(p, s, t), out_sent.at[p, s], out_came.at[p, s], fsdp=s)

    def to_mate(p, s):
        return remote(spot(p, s, t), spot(p, s, t), mate_sent.at[p, s], mate_came.at[p, s], tensor=mate)

    def to_over(p, s):
        return remote(spot(p, s, t), spot(p, s, t), over_sent.at[p, s], over_came.at[p, s], tensor=over)

    def to_relay(p, s):
        return remote(spot(p, s, over), spot(p, s, over), relay_sent.at[p, s], relay_came.at[p, s], tensor=mate)

    def own(p):
        return pltpu.make_async_copy(
            tokens_hbm.at[ds(p, rows), ds(me, depth)], columns.at[p, ds(me, rows), :], own_sem.at[p]
        )

    def forward(p):
        def go(s):
            receive_out(p, s).wait_recv()
            to_mate(p, s).start()
            to_over(p, s).start()
        each(go)

    def relay(p):
        def go(s):
            to_over(p, s).wait_recv()
            to_relay(p, s).start()
        each(go)

    def finish(p):
        own(p).wait()

        def go(s):
            to_mate(p, s).wait_recv()
            to_relay(p, s).wait_recv()
            send_out(p, s).wait_send()
            to_mate(p, s).wait_send()
            to_over(p, s).wait_send()
            to_relay(p, s).wait_send()
        each(go)

    def share(q):
        return across.at[:, :, ds(q, eighth)]

    swap = remote(
        columns.at[:, :, ds(twin * 4 + t, eighth)], share(t), swap_sem.at[0], swap_sem.at[1], replica=twin
    )
    swap_mate = remote(share(t), share(t), swap_sem.at[2], swap_sem.at[3], tensor=mate)
    swap_over = remote(share(t), share(t), swap_sem.at[4], swap_sem.at[5], tensor=over)
    swap_relay = remote(share(over), share(over), swap_sem.at[6], swap_sem.at[7], tensor=mate)

    def fetch(c):
        return pltpu.make_async_copy(codes_hbm.at[:, ds(c, width)], weight.at[c], fetched.at[c])

    def unpack(c):
        fetch(c).wait()

        def block(b, carry):
            at = ds(b, quant)
            weight[c, at, :] = (
                weight[c, at, :].astype(jnp.float32) * scales[pl.ds(b, 1), ds(c, width)]
            ).astype(jnp.bfloat16)
            return carry

        lax.fori_loop(0, depth // quant, block, 0)

    def blk(ref, s, j):
        start = s * rows if isinstance(s, int) else pl.multiple_of(s * rows, rows)
        return ref.at[j, pl.ds(start, rows), :]

    def move(source, target, s, j, sent, arrival, **device):
        return remote(blk(source, s, j), blk(target, s, j), sent.at[s, j], arrival.at[s, j], **device)

    def sum_up(d, j):
        return move(part, from_left, d, j, sum_sent, left_came, fsdp=high)

    def sum_down(d, j):
        return move(part, from_right, d, j, sum_sent, right_came, fsdp=low)

    def go_up(s, j):
        return move(mine, mine, s, j, up_sent, came, fsdp=high)

    def go_down(s, j):
        return move(mine, mine, s, j, down_sent, came, fsdp=low)

    def cross(s, j):
        return move(mine, other, s, j, cross_sent, cross_came, replica=twin)

    def act_out(j):
        at = (ds(j // chunks, rows), ds(j % chunks, width))
        return pltpu.make_async_copy(act.at[at], act_hbm.at[at], act_sem.at[j])

    def within(j):
        return jnp.logical_and(j >= 0, j < items)

    def project(j):
        part[j] = jnp.dot(
            columns[j // chunks], weight[j % chunks], preferred_element_type=jnp.float32
        ).astype(jnp.bfloat16)

    def turned_out():
        return pltpu.make_async_copy(turned, turned_hbm, turned_sem)

    def stage_out(j, which):
        return pltpu.make_async_copy(
            stage.at[j % 2, which],
            rotated_hbm.at[ds(which * parts + j // chunks, held), ds(j % chunks, width)],
            stage_sem.at[j % 2, which],
        )

    loads = (
        pltpu.make_async_copy(scales_hbm, scales, load_sem.at[0]),
        pltpu.make_async_copy(cot_hbm, cot, load_sem.at[1]),
    )
    loads[0].start()
    for c in range(2):
        fetch(c).start()
    for p in range(parts):
        own(p).start()

    barrier = pltpu.get_barrier_semaphore()
    for k in range(1, n):
        pl.semaphore_signal(barrier, inc=1, device_id={"fsdp": (me + k) % n}, device_id_type=MESH)
    for k in range(1, 4):
        pl.semaphore_signal(barrier, inc=1, device_id={"tensor": (t + k) % 4}, device_id_type=MESH)
    pl.semaphore_signal(barrier, inc=1, device_id={"replica": twin}, device_id_type=MESH)
    pl.semaphore_wait(barrier, n + 3)

    for p in range(parts):
        for k in range(1, n):
            send_out(p, (me + k) % n).start()
    for c in range(2, chunks):
        fetch(c).start()
    loads[1].start()
    loads[0].wait()

    unpack(0)
    unpack(1)
    forward(0)
    unpack(2)
    relay(0)
    unpack(3)
    finish(0)
    loads[1].wait()
    project(0)

    def chain(j, first, owners, applies, arrival, send):
        @pl.when(within(j))
        def _():
            @pl.when(jnp.logical_not(first))
            def _():
                for d in owners:
                    @pl.when(applies(d))
                    def _():
                        arrival[1](d, j).wait_recv()
                        blk(part, d, j)[...] = (
                            blk(part, d, j)[...].astype(jnp.float32)
                            + blk(arrival[0], d, j)[...].astype(jnp.float32)
                        ).astype(jnp.bfloat16)
            for d in owners:
                @pl.when(applies(d))
                def _():
                    send(d, j).start()

    def pair(p, y):
        return remote(
            whole.at[p, :, ds(2 * y + 1 - lane, piece)], pair_in.at[p, y],
            pair_sem.at[0, p, y], pair_sem.at[1, p, y], tensor=mate,
        )

    def pair_final(y):
        return remote(
            whole.at[parts - 1, ds(2 * y + 1 - lane, rows), :], pair_last.at[y],
            pair_sem.at[0, parts - 1, y], pair_sem.at[1, parts - 1, y], tensor=mate,
        )

    def flip(p):
        return remote(
            pair_sum.at[p, 1 - row], over_in.at[p], flip_sem.at[0, p], flip_sem.at[1, p], tensor=over
        )

    flip_final = remote(
        sum_last.at[1 - row], over_last, flip_sem.at[0, parts - 1], flip_sem.at[1, parts - 1], tensor=over
    )

    def line_out(p, f):
        return remote(
            quarter.at[p, ds(f, rows), :], landing.at[p, me], line_sent.at[p, f], line_came.at[p, me], fsdp=f
        )

    def line_in(p, s):
        return remote(
            landing.at[p, s], landing.at[p, s], line_sent.at[p, s], line_came.at[p, s], fsdp=s
        )

    def deal_out(p, s):
        return remote(
            landing.at[p, s], grad.at[ds(p, rows), ds(t, piece)], deal_sent.at[p, s], deal_came.at[p, t], tensor=s
        )

    def deal_in(p, q):
        at = grad.at[ds(p, rows), ds(q, piece)]
        return remote(at, at, deal_sent.at[p, q], deal_came.at[p, q], tensor=q)

    def plus(a, b):
        return (a.astype(jnp.float32) + b.astype(jnp.float32)).astype(jnp.bfloat16)

    def reduce_step(p, lag):
        @pl.when(lag == 0)
        def _():
            for y in range(2):
                pair(p, y).start()

        @pl.when(lag == 1)
        def _():
            for y in range(2):
                pair(p, y).wait()
                pair_sum[p, y] = plus(whole[p, :, ds(2 * y + lane, piece)], pair_in[p, y])
            flip(p).start()

        @pl.when(lag == 3)
        def _():
            flip(p).wait()
            quarter[p] = plus(pair_sum[p, row], over_in[p])
            landing[p, me] = quarter[p, ds(me, rows), :]
            others(me, n, lambda f: line_out(p, f).start())

        @pl.when(lag == 5)
        def _():
            def settle(s):
                line_in(p, s).wait_recv()
                line_out(p, s).wait_send()
            others(me, n, settle)
            grad[ds(p, rows), ds(t, piece)] = landing[p, t]
            others(t, 4, lambda s: deal_out(p, s).start())

        @pl.when(lag == span - 1)
        def _():
            def settle(s):
                deal_in(p, s).wait_recv()
                deal_out(p, s).wait_send()
            others(t, 4, settle)

    reach = LAG * (n - 1)

    def step(i, carry):
        up, down = i - LAG * me, i - LAG * (n - 1 - me)
        chain(up, me == 0, range(n - 1, 0, -1), lambda d: me < d, (from_left, sum_up), sum_up)
        chain(down, me == n - 1, range(n - 1), lambda d: me > d, (from_right, sum_down), sum_down)
        j = i - reach

        @pl.when(within(j))
        def _():
            total[...] = blk(part, me, j)[...].astype(jnp.float32)

            @pl.when(has_low)
            def _():
                sum_up(me, j).wait_recv()
                total[...] += blk(from_left, me, j)[...].astype(jnp.float32)

            @pl.when(has_high)
            def _():
                sum_down(me, j).wait_recv()
                total[...] += blk(from_right, me, j)[...].astype(jnp.float32)

            hidden = total[...]
            sig = jax.nn.sigmoid(hidden)
            at = (ds(j // chunks, rows), ds(j % chunks, width))
            act[at] = (hidden * sig).astype(jnp.bfloat16)
            blk(mine, me, j)[...] = (
                cot[at].astype(jnp.float32) * sig * (1.0 + hidden * (1.0 - sig))
            ).astype(jnp.bfloat16)

            @pl.when(has_high)
            def _():
                go_up(me, j).start()

            @pl.when(has_low)
            def _():
                go_down(me, j).start()

            cross(me, j).start()
            act_out(j).start()

        for k in range(1, n):
            late = i - reach - LAG * k

            @pl.when(jnp.logical_and(within(late), me - k >= 0))
            def _():
                s = me - k
                go_up(s, late).wait_recv()

                @pl.when(has_high)
                def _():
                    go_up(s, late).start()

                cross(s, late).start()

            @pl.when(jnp.logical_and(within(late), me + k < n))
            def _():
                s = me + k
                go_down(s, late).wait_recv()

                @pl.when(has_low)
                def _():
                    go_down(s, late).start()

                cross(s, late).start()

        @pl.when(jnp.logical_and(i >= 2, jnp.logical_and(i <= 2 * (parts - 1), i % 2 == 0)))
        def _():
            finish(i // 2)

        @pl.when(jnp.logical_and(i < 2 * (parts - 1), i % 2 == 0))
        def _():
            forward(1 + i // 2)

        @pl.when(jnp.logical_and(i < 2 * (parts - 1), i % 2 == 1))
        def _():
            relay(1 + i // 2)

        @pl.when(i + 4 < chunks)
        def _():
            unpack(i + 4)

        @pl.when(i + 1 < items)
        def _():
            project(i + 1)

        done = i - 2 * reach

        @pl.when(within(done))
        def _():
            c = done % chunks
            grown = lax.dot_general(
                mine[done], weight[c], (((1,), (1,)), ((), ())), preferred_element_type=jnp.float32
            )

            @pl.when(c == 0)
            def _():
                product[...] = grown

            @pl.when(c > 0)
            def _():
                product[...] += grown

            @pl.when(c == chunks - 1)
            def _():
                whole[done // chunks] = product[...].astype(jnp.bfloat16)

        age = done - (chunks - 1)

        @pl.when(jnp.logical_and(age >= 0, age // chunks < parts - 1))
        def _():
            reduce_step(age // chunks, age % chunks)

        @pl.when(i == items - 1 + 2 * reach)
        def _():
            for y in range(2):
                pair_final(y).start()

        @pl.when(i == 2 * parts)
        def _():
            swap.start()

        @pl.when(i == 2 * parts + 4)
        def _():
            swap.wait()
            swap_mate.start()
            swap_over.start()

        @pl.when(i == 2 * parts + 7)
        def _():
            swap_over.wait()
            swap_relay.start()

        @pl.when(i == 2 * parts + 10)
        def _():
            swap_mate.wait()
            swap_relay.wait()

        flat = i - (2 * parts + 11)

        @pl.when(jnp.logical_and(flat >= 0, flat < parts))
        def _():
            turned[:, ds(flat, held)] = columns[flat, :, ds(r, half)].T

        @pl.when(jnp.logical_and(flat >= parts, flat < 2 * parts))
        def _():
            turned[:, ds(flat, held)] = across[flat - parts].T

        @pl.when(flat == 2 * parts)
        def _():
            turned_out().start()

        late = i - 2 * reach - LAG

        @pl.when(within(late))
        def _():
            @pl.when(late >= 2)
            def _():
                for which in range(2):
                    stage_out(late - 2, which).wait()
            for s in range(n):
                cross(s, late).wait_recv()
            side = table_ref.shape[0]
            for which, ref in enumerate((mine, other)):
                for b in range(width // side):
                    signed = ref[late, :, b * side:(b + 1) * side] * sign_ref[
                        :, pl.ds(pl.multiple_of((late % chunks) * width + b * side, side), side)
                    ]
                    stage[late % 2, which, :, b * side:(b + 1) * side] = jnp.dot(
                        signed, table_ref[...], preferred_element_type=jnp.float32
                    ).astype(jnp.bfloat16)
            for which in range(2):
                stage_out(late, which).start()
            act_out(late).wait()
            for d in range(n):
                @pl.when(me != d)
                def _():
                    sum_up(d, late).wait_send()

                @pl.when(jnp.logical_and(has_high, me >= d))
                def _():
                    go_up(d, late).wait_send()

                @pl.when(jnp.logical_and(has_low, me <= d))
                def _():
                    go_down(d, late).wait_send()

                cross(d, late).wait_send()

        return carry

    lax.fori_loop(0, items + 2 * reach + LAG, step, 0)

    keep = grad.at[pl.ds(0, (parts - 1) * rows), :]
    grad_out = pltpu.make_async_copy(keep, grad_hbm, grad_sem)
    grad_out.start()
    for y in range(2):
        pair_final(y).wait()
        sum_last[y] = plus(whole[parts - 1, ds(2 * y + lane, rows), :], pair_last[y])
    flip_final.start()
    for j in (items - 2, items - 1):
        for which in range(2):
            stage_out(j, which).wait()
    turned_out().wait()
    grad_out.wait()
    flip_final.wait()
    last_ref[...] = plus(sum_last[row], over_last[...])


def exchange(tokens, codes, scales, cotangent, sign_bits, n, parts, width):
    local, cols = cotangent.shape
    depth = codes.shape[0]
    rows, chunks = local // parts, cols // width
    items, held, piece = parts * chunks, n * rows, depth // 4
    bf16, f32 = jnp.bfloat16, jnp.float32
    hbm = pl.BlockSpec(memory_space=pltpu.MemorySpace.HBM)
    vmem = pl.BlockSpec(memory_space=pltpu.VMEM)
    block = pltpu.VMEM((items, held, width), bf16)
    dma = pltpu.SemaphoreType.DMA
    side = 256 if width % 256 == 0 else HB
    return pl.pallas_call(
        functools.partial(exchange_kernel, n, parts, width, depth // scales.shape[0], chunks),
        out_shape=(
            jax.ShapeDtypeStruct(cotangent.shape, bf16),
            jax.ShapeDtypeStruct((depth // 2, 2 * n * local), bf16),
            jax.ShapeDtypeStruct((2 * n * local, cols), bf16),
            jax.ShapeDtypeStruct(((parts - 1) * rows, depth), bf16),
            jax.ShapeDtypeStruct((rows, depth), bf16),
        ),
        in_specs=[hbm] * 4 + [vmem] * 2,
        out_specs=(hbm,) * 4 + (vmem,),
        scratch_shapes=[
            pltpu.VMEM((parts, held, depth), bf16),
            pltpu.VMEM((parts, held, depth // 2), bf16),
            pltpu.VMEM((depth // 2, 2 * n * local), bf16),
            pltpu.VMEM((chunks, depth, width), bf16),
            pltpu.VMEM(scales.shape, f32),
            pltpu.VMEM(cotangent.shape, bf16),
            pltpu.VMEM(cotangent.shape, bf16),
        ]
        + [block] * 5
        + [
            pltpu.VMEM((2, 2, held, width), bf16),
            pltpu.VMEM((held, depth), f32),
            pltpu.VMEM((rows, width), f32),
            pltpu.VMEM((parts, held, depth), bf16),
            pltpu.VMEM((parts - 1, 2, held, piece), bf16),
            pltpu.VMEM((parts - 1, 2, held, piece), bf16),
            pltpu.VMEM((parts - 1, held, piece), bf16),
            pltpu.VMEM((parts - 1, held, piece), bf16),
            pltpu.VMEM((parts - 1, n, rows, piece), bf16),
            pltpu.VMEM((local, depth), bf16),
            pltpu.VMEM((2, rows, depth), bf16),
            pltpu.VMEM((2, rows, depth), bf16),
            pltpu.VMEM((rows, depth), bf16),
            dma((2,)),
            dma((chunks,)),
            dma((parts,)),
            dma((items,)),
            dma,
            dma((2, 2)),
            dma,
        ]
        + [dma((parts, n))] * 8
        + [dma((8,))]
        + [dma((n, items))] * 8
        + [dma((2, parts, 2)), dma((2, parts))]
        + [dma((parts - 1, n))] * 2
        + [dma((parts - 1, 4))] * 2,
        compiler_params=pltpu.CompilerParams(
            collective_id=0, has_side_effects=True, vmem_limit_bytes=63 * 1024 * 1024
        ),
        name="exchange",
    )(
        tokens, codes, scales, cotangent,
        (2 * sign_bits - 1).astype(bf16)[None, :], rotation_table(side),
    )


def product_kernel(scaling, turned_ref, rotated_ref, act_ref, out_ref, act_out_ref):
    out_ref[...] = scaling * jnp.dot(turned_ref[...], rotated_ref[...], preferred_element_type=jnp.float32)
    act_out_ref[...] = act_ref[...]


def weight_product(turned, rotated, activation):
    rows, total = turned.shape
    width, local = rotated.shape[1], activation.shape[0]
    tile = next(t for t in (512, 256, HB) if width % t == 0)
    column = lambda c: (0, c)
    return pl.pallas_call(
        functools.partial(product_kernel, float(1.0 / (HB * total) ** 0.5)),
        grid=(width // tile,),
        out_shape=(
            jax.ShapeDtypeStruct((rows, width), jnp.float32),
            jax.ShapeDtypeStruct(activation.shape, activation.dtype),
        ),
        in_specs=[
            pl.BlockSpec((rows, total), lambda c: (0, 0)),
            pl.BlockSpec((total, tile), column),
            pl.BlockSpec((local, tile), column),
        ],
        out_specs=(pl.BlockSpec((rows, tile), column), pl.BlockSpec((local, tile), column)),
        compiler_params=pltpu.CompilerParams(vmem_limit_bytes=48 * 1024 * 1024),
        cost_estimate=pl.CostEstimate(
            flops=2 * rows * total * width, bytes_accessed=4 * rows * width + 2 * total * width, transcendentals=0
        ),
        name="weight_product",
    )(turned, rotated, activation)


def fits(tokens, codes, scales, cotangent, n_fsdp, n_tensor, parts, width):
    local, cols = cotangent.shape
    depth = codes.shape[0]
    if n_fsdp != 4 or n_tensor != 4 or lax.axis_size("replica") != 2:
        return False
    if local % (16 * parts) or cols % width or cols // width < 7 or depth % 1024 or (n_fsdp * local // parts) % HB:
        return False
    gathered = n_fsdp * local
    room = 2 * depth * cols + 10 * gathered * cols + 15 * gathered * depth + 4 * local * cols
    return room <= 56 * 1024 * 1024


def halve(array, keep, n_tensor, bit):
    lead = lax.dynamic_index_in_dim(array, keep, 0, keepdims=False)
    sent = lax.dynamic_index_in_dim(array, 1 - keep, 0, keepdims=False)
    came = lax.ppermute(sent, "tensor", [(t, t ^ bit) for t in range(n_tensor)])
    return (lead.astype(jnp.float32) + came.astype(jnp.float32)).astype(jnp.bfloat16)


def tensor_reduce(product, n_tensor):
    if n_tensor != 4:
        return lax.psum_scatter(product, "tensor", scatter_dimension=0, tiled=True)
    rows, cols = product.shape
    place = lax.axis_index("tensor")
    chunks = product.reshape(2, 2, rows // 4, cols).swapaxes(0, 1)
    chunks = halve(chunks, place % 2, n_tensor, 1)
    return halve(chunks, place // 2, n_tensor, 2)


def partner(array):
    return lax.ppermute(array, "replica", [(0, 1), (1, 0)])


def shards(tokens, weight_codes, scales, cotangent, sign_bits):
    n_fsdp, n_tensor = lax.axis_size("fsdp"), lax.axis_size("tensor")
    local_tokens = tokens.shape[0]
    shard_rows, hidden_cols = weight_codes.shape
    block_rows = shard_rows // scales.shape[0]
    swap = [(f * n_tensor + t, t * n_tensor + f) for f in range(n_fsdp) for t in range(n_tensor)]
    parts, width = 4, 512
    if fits(tokens, weight_codes, scales, cotangent, n_fsdp, n_tensor, parts, width):
        activation, turned, rotated, early, last = exchange(
            tokens, weight_codes, scales, cotangent, sign_bits, n_fsdp, parts, width
        )
        last = lax.ppermute(last, ("fsdp", "tensor"), swap)
        grad_codes, activation = weight_product(turned, rotated, activation)
        return (activation, jnp.concatenate([early, last], axis=0), grad_codes)
    weight = (
        (
            weight_codes.astype(jnp.float32).reshape(scales.shape[0], block_rows, hidden_cols)
            * scales[:, None, :]
        )
        .reshape(shard_rows, hidden_cols)
        .astype(jnp.bfloat16)
    )
    piece = shard_rows // n_tensor
    own = lax.dynamic_slice_in_dim(
        tokens.reshape(local_tokens, n_fsdp, shard_rows), lax.axis_index("tensor") * piece, piece, 2
    ).reshape(local_tokens, n_fsdp * piece)
    quarter = lax.all_to_all(own, "fsdp", split_axis=1, concat_axis=0, tiled=True)
    columns = lax.all_gather(quarter, "tensor", axis=1, tiled=True)
    half_rows = shard_rows // 2
    replica = lax.axis_index("replica")
    kept = lax.dynamic_slice_in_dim(columns, replica * half_rows, half_rows, 1)
    across = partner(lax.dynamic_slice_in_dim(columns, (1 - replica) * half_rows, half_rows, 1))
    hidden = lax.psum_scatter(
        jnp.dot(columns, weight, preferred_element_type=jnp.float32).astype(jnp.bfloat16),
        "fsdp",
        scatter_dimension=0,
        tiled=True,
    ).astype(jnp.float32)
    sigmoid_val = jax.nn.sigmoid(hidden)
    activation = (hidden * sigmoid_val).astype(jnp.bfloat16)
    hidden_grad = (
        cotangent.astype(jnp.float32) * sigmoid_val * (1.0 + hidden * (1.0 - sigmoid_val))
    ).astype(jnp.bfloat16)
    arrived = lax.all_gather(hidden_grad, "fsdp", axis=0, tiled=True)
    other = partner(arrived)
    product = lax.dot_general(
        arrived, weight, (((1,), (1,)), ((), ())), preferred_element_type=jnp.float32
    ).astype(jnp.bfloat16)
    turned = jnp.concatenate([kept, across], axis=0).T
    if n_fsdp == n_tensor:
        input_grad = lax.ppermute(tensor_reduce(product, n_tensor), ("fsdp", "tensor"), swap)
    else:
        returned = lax.all_to_all(product, "fsdp", split_axis=0, concat_axis=1, tiled=True)
        input_grad = lax.psum_scatter(returned, "tensor", scatter_dimension=1, tiled=True)
    grad_codes = rotated_grad(turned, arrived, other, sign_bits)
    return (activation, input_grad, grad_codes)


def solution(mesh):
    return jax.shard_map(
        shards,
        mesh=mesh,
        in_specs=(
            P(("fsdp", "replica"), None),
            P("fsdp", "tensor"),
            P("fsdp", "tensor"),
            P(("fsdp", "replica"), "tensor"),
            P("tensor"),
        ),
        out_specs=(
            P(("fsdp", "replica"), "tensor"),
            P(("fsdp", "replica"), "tensor"),
            P(("fsdp", "replica"), "tensor"),
        ),
        check_vma=False,
    )
```

```python
import functools

import jax
import jax.numpy as jnp
from jax import lax
from jax.experimental import pallas as pl
from jax.experimental.pallas import tpu as pltpu
from jax.sharding import PartitionSpec as P

HB = 128


def hadamard_table(length):
    indices = jnp.arange(length, dtype=jnp.int32)
    intersection_bits = jnp.bitwise_and(indices[:, None], indices[None, :])
    parity = jnp.zeros((length, length), jnp.int32)
    for bit_pos in range(length.bit_length() - 1):
        parity = parity + jnp.bitwise_and(jnp.right_shift(intersection_bits, bit_pos), 1)
    return (1 - 2 * (parity % 2)).astype(jnp.bfloat16)


def grad_kernel(scaling, turned_ref, mine_ref, other_ref, sign_ref, table_ref, out_ref, rotated):
    half, width = mine_ref.shape
    for part, ref in enumerate((mine_ref, other_ref)):
        for block in range(width // HB):
            cols = slice(block * HB, (block + 1) * HB)
            signed = ref[:, cols] * sign_ref[:, cols]
            rotated[part * half:(part + 1) * half, cols] = jnp.dot(
                signed, table_ref[...], preferred_element_type=jnp.float32
            ).astype(jnp.bfloat16)
    out_ref[...] = scaling * jnp.dot(turned_ref[...], rotated[...], preferred_element_type=jnp.float32)


def rotated_grad(turned, mine, other, sign_bits):
    rows, total = turned.shape
    half, width = mine.shape
    tile = next(t for t in (512, 256, HB) if width % t == 0)
    signs = (2 * sign_bits - 1).astype(jnp.bfloat16)[None, :]
    scaling = float(1.0 / (HB * total) ** 0.5)
    column = lambda c: (0, c)
    fixed = lambda c: (0, 0)
    return pl.pallas_call(
        functools.partial(grad_kernel, scaling),
        grid=(width // tile,),
        out_shape=jax.ShapeDtypeStruct((rows, width), jnp.float32),
        in_specs=[
            pl.BlockSpec((rows, total), fixed),
            pl.BlockSpec((half, tile), column),
            pl.BlockSpec((half, tile), column),
            pl.BlockSpec((1, tile), column),
            pl.BlockSpec((HB, HB), fixed),
        ],
        out_specs=pl.BlockSpec((rows, tile), column),
        scratch_shapes=[pltpu.VMEM((total, tile), jnp.bfloat16)],
        compiler_params=pltpu.CompilerParams(vmem_limit_bytes=48 * 1024 * 1024),
        cost_estimate=pl.CostEstimate(
            flops=2 * rows * total * width, bytes_accessed=4 * rows * width + 2 * total * width, transcendentals=0
        ),
        name="rotated_grad",
    )(turned, mine, other, signs, hadamard_table(HB))


MESH = pl.DeviceIdType.MESH
LAG = 2


def exchange_kernel(
    n, parts, width, quant, span,
    tokens_hbm, codes_hbm, scales_hbm, cot_hbm, bits_ref,
    act_hbm, turned_hbm, rotated_hbm, grad_hbm, last_ref,
    columns, across, turned, weight, scales, cot, act, part, from_left, from_right, mine, other,
    stage, product, total, table, signs, whole, pair_in, pair_sum, over_in, quarter, landing, grad, pair_last, sum_last, over_last,
    load_sem, fetched, own_sem, act_sem, turned_sem, stage_sem, grad_sem,
    out_came, over_came, token_sent, mate_came,
    swap_sem, came, sent, left_came, right_came, cross_came,
    pair_sem, flip_sem, line_sem, deal_sem,
):
    me, t, r = lax.axis_index("fsdp"), lax.axis_index("tensor"), lax.axis_index("replica")
    lane, row = t % 2, t // 2
    mate, over, cross_over, twin = t + 1 - 2 * lane, (t + 2) % 4, 3 - t, 1 - r
    high, low = jnp.minimum(me + 1, n - 1), jnp.maximum(me - 1, 0)
    has_low, has_high = me > 0, me < n - 1
    depth = tokens_hbm.shape[1] // n
    rows = tokens_hbm.shape[0] // parts
    piece, eighth, half = depth // 4, depth // 8, depth // 2
    chunks = weight.shape[0]
    items = parts * chunks
    held = n * rows

    def ds(index, size):
        return pl.ds(pl.multiple_of(index * size, size), size)

    def remote(src, dst, sent, arrival, **device):
        return pltpu.make_async_remote_copy(
            src_ref=src, dst_ref=dst, send_sem=sent, recv_sem=arrival, device_id=device, device_id_type=MESH
        )

    def each(act_on):
        for k in range(1, n):
            for s in (me - k, me + k):
                @pl.when(jnp.logical_and(s >= 0, s < n))
                def _():
                    act_on(s)

    def others(index, count, act_on):
        for k in range(count):
            @pl.when(index != k)
            def _():
                act_on(k)

    def spot(p, s, q):
        return columns.at[p, ds(s, rows), ds(q, piece)]

    def send_out(p, f):
        return remote(
            tokens_hbm.at[ds(p, rows), ds(f * 4 + t, piece)], spot(p, me, t),
            token_sent.at[p], out_came.at[p, me], fsdp=f,
        )

    def receive_out(p, s):
        return remote(spot(p, s, t), spot(p, s, t), token_sent.at[p], out_came.at[p, s], fsdp=s)

    def to_mate(p, s):
        return remote(spot(p, s, t), spot(p, s, t), token_sent.at[p], mate_came.at[p], tensor=mate)

    def to_over(p, s):
        return remote(spot(p, s, t), spot(p, s, t), token_sent.at[p], over_came.at[p, s], tensor=over)

    def to_relay(p, s):
        return remote(spot(p, s, over), spot(p, s, over), token_sent.at[p], mate_came.at[p], tensor=mate)

    def own(p):
        return pltpu.make_async_copy(
            tokens_hbm.at[ds(p, rows), ds(me, depth)], columns.at[p, ds(me, rows), :], own_sem.at[p]
        )

    def forward(p):
        def go(s):
            receive_out(p, s).wait_recv()
            to_mate(p, s).start()
            to_over(p, s).start()
        each(go)

    def relay(p):
        def go(s):
            to_over(p, s).wait_recv()
            to_relay(p, s).start()
        each(go)

    def finish(p):
        own(p).wait()
        lead = columns.at[p, pl.ds(0, (n - 1) * rows), :]
        two = columns.at[p, pl.ds(0, (n - 1) * rows), pl.ds(0, 2 * piece)]
        remote(two, two, token_sent.at[p], mate_came.at[p], tensor=mate).wait_recv()
        remote(lead, lead, token_sent.at[p], mate_came.at[p], tensor=mate).wait_send()

    def share(q):
        return across.at[:, :, ds(q, eighth)]

    swap = remote(
        columns.at[:, :, ds(twin * 4 + t, eighth)], share(t), swap_sem.at[0], swap_sem.at[1], replica=twin
    )
    swap_mate = remote(share(t), share(t), swap_sem.at[2], swap_sem.at[3], tensor=mate)
    swap_over = remote(share(t), share(t), swap_sem.at[4], swap_sem.at[5], tensor=over)
    swap_relay = remote(share(over), share(over), swap_sem.at[6], swap_sem.at[7], tensor=mate)

    def fetch(c):
        return pltpu.make_async_copy(codes_hbm.at[:, ds(c, width)], weight.at[c], fetched.at[c])

    def unpack(c):
        fetch(c).wait()

        def block(b, carry):
            at = ds(b, quant)
            weight[c, at, :] = (
                weight[c, at, :].astype(jnp.float32) * scales[pl.ds(b, 1), ds(c, width)]
            ).astype(jnp.bfloat16)
            return carry

        lax.fori_loop(0, depth // quant, block, 0)

    def blk(ref, s, j):
        start = s * rows if isinstance(s, int) else pl.multiple_of(s * rows, rows)
        return ref.at[j, pl.ds(start, rows), :]

    def span_of(ref, j, start, count):
        return ref.at[j, pl.ds(start * rows, count * rows), :]

    def sum_up(m, j):
        at = (j, m + 1, n - 1 - m)
        return remote(span_of(part, *at), span_of(from_left, *at), sent.at[j], left_came.at[j], fsdp=high)

    def sum_down(m, j):
        at = (j, 0, m)
        return remote(span_of(part, *at), span_of(from_right, *at), sent.at[j], right_came.at[j], fsdp=low)

    def move(target, s, j, arrival, **device):
        return remote(blk(mine, s, j), blk(target, s, j), sent.at[j], arrival, **device)

    def go_up(s, j):
        return move(mine, s, j, came.at[s, j], fsdp=high)

    def go_down(s, j):
        return move(mine, s, j, came.at[s, j], fsdp=low)

    def cross(s, j):
        return move(other, s, j, cross_came.at[j], replica=twin)

    def act_out(p):
        at = act.at[ds(p, rows), :]
        return pltpu.make_async_copy(at, act_hbm.at[ds(p, rows), :], act_sem.at[p])

    def within(j):
        return jnp.logical_and(j >= 0, j < items)

    def project(j):
        part[j] = jnp.dot(
            columns[j // chunks], weight[j % chunks], preferred_element_type=jnp.float32
        ).astype(jnp.bfloat16)

    def turned_out():
        return pltpu.make_async_copy(turned, turned_hbm, turned_sem)

    def stage_out(j, which):
        return pltpu.make_async_copy(
            stage.at[j % 2, which],
            rotated_hbm.at[ds(which * parts + j // chunks, held), ds(j % chunks, width)],
            stage_sem.at[j % 2, which],
        )

    loads = (
        pltpu.make_async_copy(scales_hbm, scales, load_sem.at[0]),
        pltpu.make_async_copy(cot_hbm, cot, load_sem.at[1]),
    )
    loads[0].start()
    for c in range(2):
        fetch(c).start()
    for p in range(parts):
        own(p).start()

    barrier = pltpu.get_barrier_semaphore()
    for k in range(1, n):
        pl.semaphore_signal(barrier, inc=1, device_id={"fsdp": (me + k) % n}, device_id_type=MESH)
    for k in range(1, 4):
        pl.semaphore_signal(barrier, inc=1, device_id={"tensor": (t + k) % 4}, device_id_type=MESH)
    pl.semaphore_signal(barrier, inc=1, device_id={"replica": twin}, device_id_type=MESH)
    pl.semaphore_wait(barrier, n + 3)

    for p in range(parts):
        for k in range(1, n):
            send_out(p, (me + k) % n).start()
    for c in range(2, chunks):
        fetch(c).start()
    loads[1].start()
    side = table.shape[0]
    first_index = lax.broadcasted_iota(jnp.int32, (side, side), 0)
    second_index = lax.broadcasted_iota(jnp.int32, (side, side), 1)
    parity = jnp.bitwise_and(jnp.bitwise_and(first_index, second_index), HB - 1)
    for shift in (4, 2, 1):
        parity = jnp.bitwise_xor(parity, jnp.right_shift(parity, shift))
    entry = (1 - 2 * jnp.bitwise_and(parity, 1)).astype(jnp.float32)
    table[...] = jnp.where(jnp.bitwise_xor(first_index, second_index) < HB, entry, 0.0).astype(jnp.bfloat16)
    for b in range(bits_ref.shape[0]):
        signs[:, b * HB:(b + 1) * HB] = (2 * bits_ref[b:b + 1, :] - 1).astype(jnp.float32)
    loads[0].wait()

    unpack(0)
    unpack(1)
    forward(0)
    unpack(2)
    relay(0)
    unpack(3)
    finish(0)
    loads[1].wait()
    project(0)

    def plus(a, b):
        return (a.astype(jnp.float32) + b.astype(jnp.float32)).astype(jnp.bfloat16)

    def chain_up(m, j):
        if m > 0:
            sum_up(m - 1, j).wait_recv()
        if m < n - 1:
            if m > 0:
                at = pl.ds((m + 1) * rows, (n - 1 - m) * rows)
                part[j, at, :] = plus(part[j, at, :], from_left[j, at, :])
            sum_up(m, j).start()

    def chain_down(m, j):
        if m < n - 1:
            sum_down(m + 1, j).wait_recv()
        if m > 0:
            if m < n - 1:
                at = pl.ds(0, m * rows)
                part[j, at, :] = plus(part[j, at, :], from_right[j, at, :])
            sum_down(m, j).start()

    def pair(p, y):
        return remote(
            whole.at[p, :, ds(2 * y + 1 - lane, piece)], pair_in.at[p, y],
            pair_sem.at[0, p], pair_sem.at[1, p], tensor=mate,
        )

    def pair_final(y):
        return remote(
            whole.at[parts - 1, ds(2 * y + 1 - lane, rows), :], pair_last.at[y],
            pair_sem.at[0, parts - 1], pair_sem.at[1, parts - 1], tensor=mate,
        )

    def flip(p):
        return remote(
            pair_sum.at[p, 1 - row], over_in.at[p], flip_sem.at[0, p], flip_sem.at[1, p], tensor=over
        )

    flip_final = remote(
        sum_last.at[1 - row], over_last, flip_sem.at[0, parts - 1], flip_sem.at[1, parts - 1], tensor=over
    )

    def line_out(p, f):
        return remote(
            quarter.at[p, ds(f, rows), :], landing.at[p, me], line_sem.at[0, p], line_sem.at[1, p], fsdp=f
        )

    def line_all(p):
        at = landing.at[p, pl.ds(0, n - 1)]
        return remote(at, at, line_sem.at[0, p], line_sem.at[1, p], fsdp=high)

    def deal_out(p, s):
        return remote(
            landing.at[p, s], grad.at[ds(p, rows), ds(t, piece)], deal_sem.at[0, p], deal_sem.at[1, p], tensor=s
        )

    def deal_all(p):
        at = landing.at[p, pl.ds(0, 3)]
        return remote(at, at, deal_sem.at[0, p], deal_sem.at[1, p], tensor=mate)

    def reduce_step(p, lag):
        @pl.when(lag == 0)
        def _():
            for y in range(2):
                pair(p, y).start()

        @pl.when(lag == 1)
        def _():
            remote(pair_in.at[p], pair_in.at[p], pair_sem.at[0, p], pair_sem.at[1, p], tensor=mate).wait()
            for y in range(2):
                pair_sum[p, y] = plus(whole[p, :, ds(2 * y + lane, piece)], pair_in[p, y])
            flip(p).start()

        @pl.when(lag == 3)
        def _():
            flip(p).wait()
            quarter[p] = plus(pair_sum[p, row], over_in[p])
            landing[p, me] = quarter[p, ds(me, rows), :]
            others(me, n, lambda f: line_out(p, f).start())

        @pl.when(lag == 5)
        def _():
            line_all(p).wait()
            grad[ds(p, rows), ds(t, piece)] = landing[p, t]
            others(t, 4, lambda s: deal_out(p, s).start())

        @pl.when(lag == span - 1)
        def _():
            deal_all(p).wait()

    reach = LAG * (n - 1)

    def step(i, carry):
        for m in range(n):
            up, down = i - LAG * m, i - LAG * (n - 1 - m)

            @pl.when(jnp.logical_and(me == m, within(up)))
            def _():
                chain_up(m, up)

            @pl.when(jnp.logical_and(me == m, within(down)))
            def _():
                chain_down(m, down)

        j = i - reach

        @pl.when(within(j))
        def _():
            total[...] = blk(part, me, j)[...].astype(jnp.float32)

            @pl.when(has_low)
            def _():
                total[...] += blk(from_left, me, j)[...].astype(jnp.float32)

            @pl.when(has_high)
            def _():
                total[...] += blk(from_right, me, j)[...].astype(jnp.float32)

            hidden = total[...]
            sig = jax.nn.sigmoid(hidden)
            at = (ds(j // chunks, rows), ds(j % chunks, width))
            act[at] = (hidden * sig).astype(jnp.bfloat16)
            blk(mine, me, j)[...] = (
                cot[at].astype(jnp.float32) * sig * (1.0 + hidden * (1.0 - sig))
            ).astype(jnp.bfloat16)

            @pl.when(has_high)
            def _():
                go_up(me, j).start()

            @pl.when(has_low)
            def _():
                go_down(me, j).start()

            cross(me, j).start()

            @pl.when(j % chunks == chunks - 1)
            def _():
                act_out(j // chunks).start()

        for k in range(1, n):
            late = i - reach - LAG * k

            @pl.when(jnp.logical_and(within(late), me - k >= 0))
            def _():
                s = me - k
                go_up(s, late).wait_recv()

                @pl.when(has_high)
                def _():
                    go_up(s, late).start()

                cross(s, late).start()

            @pl.when(jnp.logical_and(within(late), me + k < n))
            def _():
                s = me + k
                go_down(s, late).wait_recv()

                @pl.when(has_low)
                def _():
                    go_down(s, late).start()

                cross(s, late).start()

        @pl.when(jnp.logical_and(i >= 2, jnp.logical_and(i <= 2 * (parts - 1), i % 2 == 0)))
        def _():
            finish(i // 2)

        @pl.when(jnp.logical_and(i < 2 * (parts - 1), i % 2 == 0))
        def _():
            forward(1 + i // 2)

        @pl.when(jnp.logical_and(i < 2 * (parts - 1), i % 2 == 1))
        def _():
            relay(1 + i // 2)

        @pl.when(i + 4 < chunks)
        def _():
            unpack(i + 4)

        @pl.when(i + 1 < items)
        def _():
            project(i + 1)

        done = i - 2 * reach

        @pl.when(within(done))
        def _():
            c = done % chunks
            grown = lax.dot_general(
                mine[done], weight[c], (((1,), (1,)), ((), ())), preferred_element_type=jnp.float32
            )

            @pl.when(c == 0)
            def _():
                product[...] = grown

            @pl.when(c > 0)
            def _():
                product[...] += grown

            @pl.when(c == chunks - 1)
            def _():
                whole[done // chunks] = product[...].astype(jnp.bfloat16)

        age = done - (chunks - 1)

        @pl.when(jnp.logical_and(age >= 0, age // chunks < parts - 1))
        def _():
            reduce_step(age // chunks, age % chunks)

        @pl.when(i == items - 1 + 2 * reach)
        def _():
            for y in range(2):
                pair_final(y).start()

        @pl.when(i == 2 * parts)
        def _():
            swap.start()

        @pl.when(i == 2 * parts + 4)
        def _():
            swap.wait()
            swap_mate.start()
            swap_over.start()

        @pl.when(i == 2 * parts + 7)
        def _():
            swap_over.wait()
            swap_relay.start()

        @pl.when(i == 2 * parts + 10)
        def _():
            swap_mate.wait()
            swap_relay.wait()

        flat = i - (2 * parts + 11)

        @pl.when(jnp.logical_and(flat >= 0, flat < parts))
        def _():
            turned[:, ds(flat, held)] = columns[flat, :, ds(r, half)].T

        @pl.when(jnp.logical_and(flat >= parts, flat < 2 * parts))
        def _():
            turned[:, ds(flat, held)] = across[flat - parts].T

        @pl.when(flat == 2 * parts)
        def _():
            turned_out().start()

        late = i - 2 * reach - LAG

        @pl.when(within(late))
        def _():
            @pl.when(late >= 2)
            def _():
                for which in range(2):
                    stage_out(late - 2, which).wait()
            remote(mine.at[late], other.at[late], sent.at[late], cross_came.at[late], replica=twin).wait_recv()
            for which, ref in enumerate((mine, other)):
                for b in range(width // side):
                    signed = (
                        ref[late, :, b * side:(b + 1) * side].astype(jnp.float32)
                        * signs[:, pl.ds(pl.multiple_of((late % chunks) * width + b * side, side), side)]
                    ).astype(jnp.bfloat16)
                    stage[late % 2, which, :, b * side:(b + 1) * side] = jnp.dot(
                        signed, table[...], preferred_element_type=jnp.float32
                    ).astype(jnp.bfloat16)
            for which in range(2):
                stage_out(late, which).start()

            def sent_all(count):
                at = mine.at[pl.ds(0, count)]
                remote(at, at, sent.at[late], cross_came.at[late], replica=twin).wait_send()

            at_end = jnp.logical_or(me == 0, me == n - 1)

            @pl.when(at_end)
            def _():
                sent_all(2)

            @pl.when(jnp.logical_not(at_end))
            def _():
                sent_all(3)

        return carry

    lax.fori_loop(0, items + 2 * reach + LAG, step, 0)

    keep = grad.at[pl.ds(0, (parts - 1) * rows), :]
    grad_out = pltpu.make_async_copy(keep, grad_hbm, grad_sem)
    grad_out.start()
    remote(
        pair_last, pair_last, pair_sem.at[0, parts - 1], pair_sem.at[1, parts - 1], tensor=mate
    ).wait()
    for y in range(2):
        sum_last[y] = plus(whole[parts - 1, ds(2 * y + lane, rows), :], pair_last[y])
    flip_final.start()
    for j in (items - 2, items - 1):
        for which in range(2):
            stage_out(j, which).wait()
    turned_out().wait()
    grad_out.wait()
    for p in range(parts):
        act_out(p).wait()
    flip_final.wait()
    last_ref[...] = plus(sum_last[row], over_last[...])


def exchange(tokens, codes, scales, cotangent, sign_bits, n, parts, width):
    local, cols = cotangent.shape
    depth = codes.shape[0]
    rows, chunks = local // parts, cols // width
    items, held, piece = parts * chunks, n * rows, depth // 4
    bf16, f32 = jnp.bfloat16, jnp.float32
    hbm = pl.BlockSpec(memory_space=pltpu.MemorySpace.HBM)
    vmem = pl.BlockSpec(memory_space=pltpu.VMEM)
    block = pltpu.VMEM((items, held, width), bf16)
    dma = pltpu.SemaphoreType.DMA
    side = 256 if width % 256 == 0 else HB
    return pl.pallas_call(
        functools.partial(exchange_kernel, n, parts, width, depth // scales.shape[0], chunks),
        out_shape=(
            jax.ShapeDtypeStruct(cotangent.shape, bf16),
            jax.ShapeDtypeStruct((depth // 2, 2 * n * local), bf16),
            jax.ShapeDtypeStruct((2 * n * local, cols), bf16),
            jax.ShapeDtypeStruct(((parts - 1) * rows, depth), bf16),
            jax.ShapeDtypeStruct((rows, depth), bf16),
        ),
        in_specs=[hbm] * 4 + [vmem],
        out_specs=(hbm,) * 4 + (vmem,),
        scratch_shapes=[
            pltpu.VMEM((parts, held, depth), bf16),
            pltpu.VMEM((parts, held, depth // 2), bf16),
            pltpu.VMEM((depth // 2, 2 * n * local), bf16),
            pltpu.VMEM((chunks, depth, width), bf16),
            pltpu.VMEM(scales.shape, f32),
            pltpu.VMEM(cotangent.shape, bf16),
            pltpu.VMEM(cotangent.shape, bf16),
        ]
        + [block] * 5
        + [
            pltpu.VMEM((2, 2, held, width), bf16),
            pltpu.VMEM((held, depth), f32),
            pltpu.VMEM((rows, width), f32),
            pltpu.VMEM((side, side), bf16),
            pltpu.VMEM((1, cols), f32),
            pltpu.VMEM((parts, held, depth), bf16),
            pltpu.VMEM((parts - 1, 2, held, piece), bf16),
            pltpu.VMEM((parts - 1, 2, held, piece), bf16),
            pltpu.VMEM((parts - 1, held, piece), bf16),
            pltpu.VMEM((parts - 1, held, piece), bf16),
            pltpu.VMEM((parts - 1, n, rows, piece), bf16),
            pltpu.VMEM((local, depth), bf16),
            pltpu.VMEM((2, rows, depth), bf16),
            pltpu.VMEM((2, rows, depth), bf16),
            pltpu.VMEM((rows, depth), bf16),
            dma((2,)),
            dma((chunks,)),
            dma((parts,)),
            dma((parts,)),
            dma,
            dma((2, 2)),
            dma,
        ]
        + [dma((parts, n))] * 2
        + [dma((parts,))] * 2
        + [dma((8,))]
        + [dma((n, items))]
        + [dma((items,))] * 4
        + [dma((2, parts))] * 2
        + [dma((2, parts - 1))] * 2,
        compiler_params=pltpu.CompilerParams(
            collective_id=0, has_side_effects=True, vmem_limit_bytes=63 * 1024 * 1024
        ),
        name="exchange",
    )(tokens, codes, scales, cotangent, sign_bits.reshape(cols // HB, HB))


def product_kernel(scaling, turned_ref, rotated_ref, act_ref, out_ref, act_out_ref):
    out_ref[...] = scaling * jnp.dot(turned_ref[...], rotated_ref[...], preferred_element_type=jnp.float32)
    act_out_ref[...] = act_ref[...]


def weight_product(turned, rotated, activation):
    rows, total = turned.shape
    width, local = rotated.shape[1], activation.shape[0]
    tile = next(t for t in (512, 256, HB) if width % t == 0)
    column = lambda c: (0, c)
    return pl.pallas_call(
        functools.partial(product_kernel, float(1.0 / (HB * total) ** 0.5)),
        grid=(width // tile,),
        out_shape=(
            jax.ShapeDtypeStruct((rows, width), jnp.float32),
            jax.ShapeDtypeStruct(activation.shape, activation.dtype),
        ),
        in_specs=[
            pl.BlockSpec((rows, total), lambda c: (0, 0)),
            pl.BlockSpec((total, tile), column),
            pl.BlockSpec((local, tile), column),
        ],
        out_specs=(pl.BlockSpec((rows, tile), column), pl.BlockSpec((local, tile), column)),
        compiler_params=pltpu.CompilerParams(vmem_limit_bytes=63 * 1024 * 1024),
        cost_estimate=pl.CostEstimate(
            flops=2 * rows * total * width, bytes_accessed=4 * rows * width + 2 * total * width, transcendentals=0
        ),
        name="weight_product",
    )(turned, rotated, activation)


def fits(tokens, codes, scales, cotangent, n_fsdp, n_tensor, parts, width):
    local, cols = cotangent.shape
    depth = codes.shape[0]
    if n_fsdp != 4 or n_tensor != 4 or lax.axis_size("replica") != 2:
        return False
    if local % (16 * parts) or cols % width or cols // width < 7 or depth % 1024 or (n_fsdp * local // parts) % HB:
        return False
    gathered = n_fsdp * local
    room = 2 * depth * cols + 10 * gathered * cols + 15 * gathered * depth + 4 * local * cols
    return room <= 56 * 1024 * 1024


def halve(array, keep, n_tensor, bit):
    lead = lax.dynamic_index_in_dim(array, keep, 0, keepdims=False)
    sent = lax.dynamic_index_in_dim(array, 1 - keep, 0, keepdims=False)
    came = lax.ppermute(sent, "tensor", [(t, t ^ bit) for t in range(n_tensor)])
    return (lead.astype(jnp.float32) + came.astype(jnp.float32)).astype(jnp.bfloat16)


def tensor_reduce(product, n_tensor):
    if n_tensor != 4:
        return lax.psum_scatter(product, "tensor", scatter_dimension=0, tiled=True)
    rows, cols = product.shape
    place = lax.axis_index("tensor")
    chunks = product.reshape(2, 2, rows // 4, cols).swapaxes(0, 1)
    chunks = halve(chunks, place % 2, n_tensor, 1)
    return halve(chunks, place // 2, n_tensor, 2)


def partner(array):
    return lax.ppermute(array, "replica", [(0, 1), (1, 0)])


def shards(tokens, weight_codes, scales, cotangent, sign_bits):
    n_fsdp, n_tensor = lax.axis_size("fsdp"), lax.axis_size("tensor")
    local_tokens = tokens.shape[0]
    shard_rows, hidden_cols = weight_codes.shape
    block_rows = shard_rows // scales.shape[0]
    swap = [(f * n_tensor + t, t * n_tensor + f) for f in range(n_fsdp) for t in range(n_tensor)]
    parts, width = 4, 512
    if fits(tokens, weight_codes, scales, cotangent, n_fsdp, n_tensor, parts, width):
        activation, turned, rotated, early, last = exchange(
            tokens, weight_codes, scales, cotangent, sign_bits, n_fsdp, parts, width
        )
        last = lax.ppermute(last, ("fsdp", "tensor"), swap)
        grad_codes, activation = weight_product(turned, rotated, activation)
        return (activation, jnp.concatenate([early, last], axis=0), grad_codes)
    weight = (
        (
            weight_codes.astype(jnp.float32).reshape(scales.shape[0], block_rows, hidden_cols)
            * scales[:, None, :]
        )
        .reshape(shard_rows, hidden_cols)
        .astype(jnp.bfloat16)
    )
    piece = shard_rows // n_tensor
    own = lax.dynamic_slice_in_dim(
        tokens.reshape(local_tokens, n_fsdp, shard_rows), lax.axis_index("tensor") * piece, piece, 2
    ).reshape(local_tokens, n_fsdp * piece)
    quarter = lax.all_to_all(own, "fsdp", split_axis=1, concat_axis=0, tiled=True)
    columns = lax.all_gather(quarter, "tensor", axis=1, tiled=True)
    half_rows = shard_rows // 2
    replica = lax.axis_index("replica")
    kept = lax.dynamic_slice_in_dim(columns, replica * half_rows, half_rows, 1)
    across = partner(lax.dynamic_slice_in_dim(columns, (1 - replica) * half_rows, half_rows, 1))
    hidden = lax.psum_scatter(
        jnp.dot(columns, weight, preferred_element_type=jnp.float32).astype(jnp.bfloat16),
        "fsdp",
        scatter_dimension=0,
        tiled=True,
    ).astype(jnp.float32)
    sigmoid_val = jax.nn.sigmoid(hidden)
    activation = (hidden * sigmoid_val).astype(jnp.bfloat16)
    hidden_grad = (
        cotangent.astype(jnp.float32) * sigmoid_val * (1.0 + hidden * (1.0 - sigmoid_val))
    ).astype(jnp.bfloat16)
    arrived = lax.all_gather(hidden_grad, "fsdp", axis=0, tiled=True)
    other = partner(arrived)
    product = lax.dot_general(
        arrived, weight, (((1,), (1,)), ((), ())), preferred_element_type=jnp.float32
    ).astype(jnp.bfloat16)
    turned = jnp.concatenate([kept, across], axis=0).T
    if n_fsdp == n_tensor:
        input_grad = lax.ppermute(tensor_reduce(product, n_tensor), ("fsdp", "tensor"), swap)
    else:
        returned = lax.all_to_all(product, "fsdp", split_axis=0, concat_axis=1, tiled=True)
        input_grad = lax.psum_scatter(returned, "tensor", scatter_dimension=1, tiled=True)
    grad_codes = rotated_grad(turned, arrived, other, sign_bits)
    return (activation, input_grad, grad_codes)


def solution(mesh):
    return jax.shard_map(
        shards,
        mesh=mesh,
        in_specs=(
            P(("fsdp", "replica"), None),
            P("fsdp", "tensor"),
            P("fsdp", "tensor"),
            P(("fsdp", "replica"), "tensor"),
            P("tensor"),
        ),
        out_specs=(
            P(("fsdp", "replica"), "tensor"),
            P(("fsdp", "replica"), "tensor"),
            P(("fsdp", "replica"), "tensor"),
        ),
        check_vma=False,
    )
```

```python
import functools

import jax
import jax.numpy as jnp
from jax import lax
from jax.experimental import pallas as pl
from jax.experimental.pallas import tpu as pltpu
from jax.sharding import PartitionSpec as P

HB = 128


def hadamard_table(length):
    indices = jnp.arange(length, dtype=jnp.int32)
    intersection_bits = jnp.bitwise_and(indices[:, None], indices[None, :])
    parity = jnp.zeros((length, length), jnp.int32)
    for bit_pos in range(length.bit_length() - 1):
        parity = parity + jnp.bitwise_and(jnp.right_shift(intersection_bits, bit_pos), 1)
    return (1 - 2 * (parity % 2)).astype(jnp.bfloat16)


def grad_kernel(scaling, turned_ref, mine_ref, other_ref, sign_ref, table_ref, out_ref, rotated):
    half, width = mine_ref.shape
    for part, ref in enumerate((mine_ref, other_ref)):
        for block in range(width // HB):
            cols = slice(block * HB, (block + 1) * HB)
            signed = ref[:, cols] * sign_ref[:, cols]
            rotated[part * half:(part + 1) * half, cols] = jnp.dot(
                signed, table_ref[...], preferred_element_type=jnp.float32
            ).astype(jnp.bfloat16)
    out_ref[...] = scaling * jnp.dot(turned_ref[...], rotated[...], preferred_element_type=jnp.float32)


def rotated_grad(turned, mine, other, sign_bits):
    rows, total = turned.shape
    half, width = mine.shape
    tile = next(t for t in (512, 256, HB) if width % t == 0)
    signs = (2 * sign_bits - 1).astype(jnp.bfloat16)[None, :]
    scaling = float(1.0 / (HB * total) ** 0.5)
    column = lambda c: (0, c)
    fixed = lambda c: (0, 0)
    return pl.pallas_call(
        functools.partial(grad_kernel, scaling),
        grid=(width // tile,),
        out_shape=jax.ShapeDtypeStruct((rows, width), jnp.float32),
        in_specs=[
            pl.BlockSpec((rows, total), fixed),
            pl.BlockSpec((half, tile), column),
            pl.BlockSpec((half, tile), column),
            pl.BlockSpec((1, tile), column),
            pl.BlockSpec((HB, HB), fixed),
        ],
        out_specs=pl.BlockSpec((rows, tile), column),
        scratch_shapes=[pltpu.VMEM((total, tile), jnp.bfloat16)],
        compiler_params=pltpu.CompilerParams(vmem_limit_bytes=48 * 1024 * 1024),
        cost_estimate=pl.CostEstimate(
            flops=2 * rows * total * width, bytes_accessed=4 * rows * width + 2 * total * width, transcendentals=0
        ),
        name="rotated_grad",
    )(turned, mine, other, signs, hadamard_table(HB))


MESH = pl.DeviceIdType.MESH
LAG = 2


def exchange_kernel(
    n, parts, width, quant, span,
    tokens_hbm, codes_hbm, scales_hbm, cot_hbm, bits_ref,
    act_hbm, turned_hbm, rotated_hbm, grad_hbm, last_ref,
    columns, across, turned, weight, scales, cot, act, part, from_left, from_right, mine, other,
    stage, product, total, table, signs, whole, pair_in, pair_sum, over_in, quarter, landing, grad, pair_last, sum_last, over_last,
    load_sem, fetched, own_sem, act_sem, turned_sem, stage_sem, grad_sem,
    out_came, over_came, token_sent, mate_came,
    swap_sem, came, sent, left_came, right_came, cross_came,
    pair_sem, flip_sem, line_sem, deal_sem,
):
    me, t, r = lax.axis_index("fsdp"), lax.axis_index("tensor"), lax.axis_index("replica")
    lane, row = t % 2, t // 2
    mate, over, cross_over, twin = t + 1 - 2 * lane, (t + 2) % 4, 3 - t, 1 - r
    high, low = jnp.minimum(me + 1, n - 1), jnp.maximum(me - 1, 0)
    has_low, has_high = me > 0, me < n - 1
    depth = tokens_hbm.shape[1] // n
    rows = tokens_hbm.shape[0] // parts
    piece, eighth, half = depth // 4, depth // 8, depth // 2
    chunks = weight.shape[0]
    items = parts * chunks
    held = n * rows

    def ds(index, size):
        return pl.ds(pl.multiple_of(index * size, size), size)

    def remote(src, dst, sent, arrival, **device):
        return pltpu.make_async_remote_copy(
            src_ref=src, dst_ref=dst, send_sem=sent, recv_sem=arrival, device_id=device, device_id_type=MESH
        )

    def each(act_on):
        for k in range(1, n):
            for s in (me - k, me + k):
                @pl.when(jnp.logical_and(s >= 0, s < n))
                def _():
                    act_on(s)

    def others(index, count, act_on):
        for k in range(count):
            @pl.when(index != k)
            def _():
                act_on(k)

    def spot(p, s, q):
        return columns.at[p, ds(s, rows), ds(q, piece)]

    def send_out(p, f):
        return remote(
            tokens_hbm.at[ds(p, rows), ds(f * 4 + t, piece)], spot(p, me, t),
            token_sent.at[p], out_came.at[p, me], fsdp=f,
        )

    def receive_out(p, s):
        return remote(spot(p, s, t), spot(p, s, t), token_sent.at[p], out_came.at[p, s], fsdp=s)

    def to_mate(p, s):
        return remote(spot(p, s, t), spot(p, s, t), token_sent.at[p], mate_came.at[p], tensor=mate)

    def to_over(p, s):
        return remote(spot(p, s, t), spot(p, s, t), token_sent.at[p], over_came.at[p, s], tensor=over)

    def to_relay(p, s):
        return remote(spot(p, s, over), spot(p, s, over), token_sent.at[p], mate_came.at[p], tensor=mate)

    def own(p):
        return pltpu.make_async_copy(
            tokens_hbm.at[ds(p, rows), ds(me, depth)], columns.at[p, ds(me, rows), :], own_sem.at[p]
        )

    def forward(p):
        def go(s):
            receive_out(p, s).wait_recv()
            to_mate(p, s).start()
            to_over(p, s).start()
        each(go)

    def relay(p):
        def go(s):
            to_over(p, s).wait_recv()
            to_relay(p, s).start()
        each(go)

    def finish(p):
        own(p).wait()
        lead = columns.at[p, pl.ds(0, (n - 1) * rows), :]
        two = columns.at[p, pl.ds(0, (n - 1) * rows), pl.ds(0, 2 * piece)]
        remote(two, two, token_sent.at[p], mate_came.at[p], tensor=mate).wait_recv()
        remote(lead, lead, token_sent.at[p], mate_came.at[p], tensor=mate).wait_send()

    def share(q):
        return across.at[:, :, ds(q, eighth)]

    swap = remote(
        columns.at[:, :, ds(twin * 4 + t, eighth)], share(t), swap_sem.at[0], swap_sem.at[1], replica=twin
    )
    swap_mate = remote(share(t), share(t), swap_sem.at[2], swap_sem.at[3], tensor=mate)
    swap_over = remote(share(t), share(t), swap_sem.at[4], swap_sem.at[5], tensor=over)
    swap_relay = remote(share(over), share(over), swap_sem.at[6], swap_sem.at[7], tensor=mate)

    def fetch(c):
        return pltpu.make_async_copy(codes_hbm.at[:, ds(c, width)], weight.at[c], fetched.at[c])

    def unpack(c):
        fetch(c).wait()

        def block(b, carry):
            at = ds(b, quant)
            weight[c, at, :] = (
                weight[c, at, :].astype(jnp.float32) * scales[pl.ds(b, 1), ds(c, width)]
            ).astype(jnp.bfloat16)
            return carry

        lax.fori_loop(0, depth // quant, block, 0)

    def blk(ref, s, j):
        start = s * rows if isinstance(s, int) else pl.multiple_of(s * rows, rows)
        return ref.at[j, pl.ds(start, rows), :]

    def span_of(ref, j, start, count):
        return ref.at[j, pl.ds(start * rows, count * rows), :]

    def sum_up(m, j):
        at = (j, m + 1, n - 1 - m)
        return remote(span_of(part, *at), span_of(from_left, *at), sent.at[j], left_came.at[j], fsdp=high)

    def sum_down(m, j):
        at = (j, 0, m)
        return remote(span_of(part, *at), span_of(from_right, *at), sent.at[j], right_came.at[j], fsdp=low)

    def move(target, s, j, arrival, **device):
        return remote(blk(mine, s, j), blk(target, s, j), sent.at[j], arrival, **device)

    def go_up(s, j):
        return move(mine, s, j, came.at[s, j], fsdp=high)

    def go_down(s, j):
        return move(mine, s, j, came.at[s, j], fsdp=low)

    def cross(s, j):
        return move(other, s, j, cross_came.at[j], replica=twin)

    def act_out(p):
        at = act.at[ds(p, rows), :]
        return pltpu.make_async_copy(at, act_hbm.at[ds(p, rows), :], act_sem.at[p])

    def within(j):
        return jnp.logical_and(j >= 0, j < items)

    def project(j):
        part[j] = jnp.dot(
            columns[j // chunks], weight[j % chunks], preferred_element_type=jnp.float32
        ).astype(jnp.bfloat16)

    def turned_out():
        return pltpu.make_async_copy(turned, turned_hbm, turned_sem)

    def stage_out(j, which):
        return pltpu.make_async_copy(
            stage.at[j % 2, which],
            rotated_hbm.at[ds(which * parts + j // chunks, held), ds(j % chunks, width)],
            stage_sem.at[j % 2, which],
        )

    loads = (
        pltpu.make_async_copy(scales_hbm, scales, load_sem.at[0]),
        pltpu.make_async_copy(cot_hbm, cot, load_sem.at[1]),
    )
    loads[0].start()
    for c in range(2):
        fetch(c).start()
    for p in range(parts):
        own(p).start()

    barrier = pltpu.get_barrier_semaphore()
    for k in range(1, n):
        pl.semaphore_signal(barrier, inc=1, device_id={"fsdp": (me + k) % n}, device_id_type=MESH)
    for k in range(1, 4):
        pl.semaphore_signal(barrier, inc=1, device_id={"tensor": (t + k) % 4}, device_id_type=MESH)
    pl.semaphore_signal(barrier, inc=1, device_id={"replica": twin}, device_id_type=MESH)
    pl.semaphore_wait(barrier, n + 3)

    for p in range(parts):
        for k in range(1, n):
            send_out(p, (me + k) % n).start()
    for c in range(2, chunks):
        fetch(c).start()
    loads[1].start()
    side = table.shape[0]
    first_index = lax.broadcasted_iota(jnp.int32, (side, side), 0)
    second_index = lax.broadcasted_iota(jnp.int32, (side, side), 1)
    parity = jnp.bitwise_and(jnp.bitwise_and(first_index, second_index), HB - 1)
    for shift in (4, 2, 1):
        parity = jnp.bitwise_xor(parity, jnp.right_shift(parity, shift))
    entry = (1 - 2 * jnp.bitwise_and(parity, 1)).astype(jnp.float32)
    table[...] = jnp.where(jnp.bitwise_xor(first_index, second_index) < HB, entry, 0.0).astype(jnp.bfloat16)
    for b in range(bits_ref.shape[0]):
        signs[:, b * HB:(b + 1) * HB] = (2 * bits_ref[b:b + 1, :] - 1).astype(jnp.float32)
    loads[0].wait()

    unpack(0)
    unpack(1)
    forward(0)
    unpack(2)
    relay(0)
    unpack(3)
    finish(0)
    loads[1].wait()
    project(0)

    def plus(a, b):
        return (a.astype(jnp.float32) + b.astype(jnp.float32)).astype(jnp.bfloat16)

    def chain_up(m, j):
        if m > 0:
            sum_up(m - 1, j).wait_recv()
        if m < n - 1:
            if m > 0:
                at = pl.ds((m + 1) * rows, (n - 1 - m) * rows)
                part[j, at, :] = plus(part[j, at, :], from_left[j, at, :])
            sum_up(m, j).start()

    def chain_down(m, j):
        if m < n - 1:
            sum_down(m + 1, j).wait_recv()
        if m > 0:
            if m < n - 1:
                at = pl.ds(0, m * rows)
                part[j, at, :] = plus(part[j, at, :], from_right[j, at, :])
            sum_down(m, j).start()

    def pair(p, y):
        return remote(
            whole.at[p, :, ds(2 * y + 1 - lane, piece)], pair_in.at[p, y],
            pair_sem.at[0, p], pair_sem.at[1, p], tensor=mate,
        )

    def pair_final(y):
        return remote(
            whole.at[parts - 1, ds(2 * y + 1 - lane, rows), :], pair_last.at[y],
            pair_sem.at[0, parts - 1], pair_sem.at[1, parts - 1], tensor=mate,
        )

    def flip(p):
        return remote(
            pair_sum.at[p, 1 - row], over_in.at[p], flip_sem.at[0, p], flip_sem.at[1, p], tensor=over
        )

    flip_final = remote(
        sum_last.at[1 - row], over_last, flip_sem.at[0, parts - 1], flip_sem.at[1, parts - 1], tensor=over
    )

    def line_out(p, f):
        return remote(
            quarter.at[p, ds(f, rows), :], landing.at[p, me], line_sem.at[0, p], line_sem.at[1, p], fsdp=f
        )

    def line_all(p):
        at = landing.at[p, pl.ds(0, n - 1)]
        return remote(at, at, line_sem.at[0, p], line_sem.at[1, p], fsdp=high)

    def deal_out(p, s):
        return remote(
            landing.at[p, s], grad.at[ds(p, rows), ds(t, piece)], deal_sem.at[0, p], deal_sem.at[1, p], tensor=s
        )

    def deal_all(p):
        at = landing.at[p, pl.ds(0, 3)]
        return remote(at, at, deal_sem.at[0, p], deal_sem.at[1, p], tensor=mate)

    def reduce_step(p, lag):
        @pl.when(lag == 0)
        def _():
            for y in range(2):
                pair(p, y).start()

        @pl.when(lag == 1)
        def _():
            remote(pair_in.at[p], pair_in.at[p], pair_sem.at[0, p], pair_sem.at[1, p], tensor=mate).wait()
            for y in range(2):
                pair_sum[p, y] = plus(whole[p, :, ds(2 * y + lane, piece)], pair_in[p, y])
            flip(p).start()

        @pl.when(lag == 3)
        def _():
            flip(p).wait()
            quarter[p] = plus(pair_sum[p, row], over_in[p])
            landing[p, me] = quarter[p, ds(me, rows), :]

    reach = LAG * (n - 1)

    def step(i, carry):
        for m in range(n):
            up, down = i - LAG * m, i - LAG * (n - 1 - m)

            @pl.when(jnp.logical_and(me == m, within(up)))
            def _():
                chain_up(m, up)

            @pl.when(jnp.logical_and(me == m, within(down)))
            def _():
                chain_down(m, down)

        j = i - reach

        @pl.when(within(j))
        def _():
            total[...] = blk(part, me, j)[...].astype(jnp.float32)

            @pl.when(has_low)
            def _():
                total[...] += blk(from_left, me, j)[...].astype(jnp.float32)

            @pl.when(has_high)
            def _():
                total[...] += blk(from_right, me, j)[...].astype(jnp.float32)

            hidden = total[...]
            sig = jax.nn.sigmoid(hidden)
            at = (ds(j // chunks, rows), ds(j % chunks, width))
            act[at] = (hidden * sig).astype(jnp.bfloat16)
            blk(mine, me, j)[...] = (
                cot[at].astype(jnp.float32) * sig * (1.0 + hidden * (1.0 - sig))
            ).astype(jnp.bfloat16)

            @pl.when(has_high)
            def _():
                go_up(me, j).start()

            @pl.when(has_low)
            def _():
                go_down(me, j).start()

            cross(me, j).start()

            @pl.when(j % chunks == chunks - 1)
            def _():
                act_out(j // chunks).start()

        for k in range(1, n):
            late = i - reach - LAG * k

            @pl.when(jnp.logical_and(within(late), me - k >= 0))
            def _():
                s = me - k
                go_up(s, late).wait_recv()

                @pl.when(has_high)
                def _():
                    go_up(s, late).start()

                cross(s, late).start()

            @pl.when(jnp.logical_and(within(late), me + k < n))
            def _():
                s = me + k
                go_down(s, late).wait_recv()

                @pl.when(has_low)
                def _():
                    go_down(s, late).start()

                cross(s, late).start()

        @pl.when(jnp.logical_and(i >= 2, jnp.logical_and(i <= 2 * (parts - 1), i % 2 == 0)))
        def _():
            finish(i // 2)

        @pl.when(jnp.logical_and(i < 2 * (parts - 1), i % 2 == 0))
        def _():
            forward(1 + i // 2)

        @pl.when(jnp.logical_and(i < 2 * (parts - 1), i % 2 == 1))
        def _():
            relay(1 + i // 2)

        @pl.when(i + 4 < chunks)
        def _():
            unpack(i + 4)

        @pl.when(i + 1 < items)
        def _():
            project(i + 1)

        done = i - 2 * reach

        @pl.when(within(done))
        def _():
            c = done % chunks
            grown = lax.dot_general(
                mine[done], weight[c], (((1,), (1,)), ((), ())), preferred_element_type=jnp.float32
            )

            @pl.when(c == 0)
            def _():
                product[...] = grown

            @pl.when(c > 0)
            def _():
                product[...] += grown

            @pl.when(c == chunks - 1)
            def _():
                whole[done // chunks] = product[...].astype(jnp.bfloat16)

        age = done - (chunks - 1)

        @pl.when(jnp.logical_and(age >= 0, age // chunks < parts - 1))
        def _():
            reduce_step(age // chunks, age % chunks)

        for p in range(parts - 1):
            begin = items + LAG * n // 2 - 1 + 2 * p

            @pl.when(i == begin)
            def _():
                others(me, n, lambda f: line_out(p, f).start())

            @pl.when(i == begin + 3)
            def _():
                line_all(p).wait()
                grad[ds(p, rows), ds(t, piece)] = landing[p, t]
                others(t, 4, lambda s: deal_out(p, s).start())

            @pl.when(i == begin + 5)
            def _():
                deal_all(p).wait()

        @pl.when(i == items - 1 + 2 * reach)
        def _():
            for y in range(2):
                pair_final(y).start()

        @pl.when(i == items + 2 * reach)
        def _():
            remote(
                pair_last, pair_last, pair_sem.at[0, parts - 1], pair_sem.at[1, parts - 1], tensor=mate
            ).wait()
            for y in range(2):
                sum_last[y] = plus(whole[parts - 1, ds(2 * y + lane, rows), :], pair_last[y])
            flip_final.start()

        @pl.when(i == 2 * parts)
        def _():
            swap.start()

        @pl.when(i == 2 * parts + 4)
        def _():
            swap.wait()
            swap_mate.start()
            swap_over.start()

        @pl.when(i == 2 * parts + 7)
        def _():
            swap_over.wait()
            swap_relay.start()

        @pl.when(i == 2 * parts + 10)
        def _():
            swap_mate.wait()
            swap_relay.wait()

        flat = i - (2 * parts + 11)

        @pl.when(jnp.logical_and(flat >= 0, flat < parts))
        def _():
            turned[:, ds(flat, held)] = columns[flat, :, ds(r, half)].T

        @pl.when(jnp.logical_and(flat >= parts, flat < 2 * parts))
        def _():
            turned[:, ds(flat, held)] = across[flat - parts].T

        @pl.when(flat == 2 * parts)
        def _():
            turned_out().start()

        late = i - 2 * reach - LAG

        @pl.when(within(late))
        def _():
            @pl.when(late >= 2)
            def _():
                for which in range(2):
                    stage_out(late - 2, which).wait()
            remote(mine.at[late], other.at[late], sent.at[late], cross_came.at[late], replica=twin).wait_recv()
            for which, ref in enumerate((mine, other)):
                for b in range(width // side):
                    signed = (
                        ref[late, :, b * side:(b + 1) * side].astype(jnp.float32)
                        * signs[:, pl.ds(pl.multiple_of((late % chunks) * width + b * side, side), side)]
                    ).astype(jnp.bfloat16)
                    stage[late % 2, which, :, b * side:(b + 1) * side] = jnp.dot(
                        signed, table[...], preferred_element_type=jnp.float32
                    ).astype(jnp.bfloat16)
            for which in range(2):
                stage_out(late, which).start()

            def sent_all(count):
                at = mine.at[pl.ds(0, count)]
                remote(at, at, sent.at[late], cross_came.at[late], replica=twin).wait_send()

            at_end = jnp.logical_or(me == 0, me == n - 1)

            @pl.when(at_end)
            def _():
                sent_all(2)

            @pl.when(jnp.logical_not(at_end))
            def _():
                sent_all(3)

        return carry

    lax.fori_loop(0, items + 2 * reach + LAG, step, 0)

    keep = grad.at[pl.ds(0, (parts - 1) * rows), :]
    grad_out = pltpu.make_async_copy(keep, grad_hbm, grad_sem)
    grad_out.start()
    for j in (items - 2, items - 1):
        for which in range(2):
            stage_out(j, which).wait()
    turned_out().wait()
    grad_out.wait()
    for p in range(parts):
        act_out(p).wait()
    flip_final.wait()
    last_ref[...] = plus(sum_last[row], over_last[...])


def exchange(tokens, codes, scales, cotangent, sign_bits, n, parts, width):
    local, cols = cotangent.shape
    depth = codes.shape[0]
    rows, chunks = local // parts, cols // width
    items, held, piece = parts * chunks, n * rows, depth // 4
    bf16, f32 = jnp.bfloat16, jnp.float32
    hbm = pl.BlockSpec(memory_space=pltpu.MemorySpace.HBM)
    vmem = pl.BlockSpec(memory_space=pltpu.VMEM)
    block = pltpu.VMEM((items, held, width), bf16)
    dma = pltpu.SemaphoreType.DMA
    side = 256 if width % 256 == 0 else HB
    return pl.pallas_call(
        functools.partial(exchange_kernel, n, parts, width, depth // scales.shape[0], chunks),
        out_shape=(
            jax.ShapeDtypeStruct(cotangent.shape, bf16),
            jax.ShapeDtypeStruct((depth // 2, 2 * n * local), bf16),
            jax.ShapeDtypeStruct((2 * n * local, cols), bf16),
            jax.ShapeDtypeStruct(((parts - 1) * rows, depth), bf16),
            jax.ShapeDtypeStruct((rows, depth), bf16),
        ),
        in_specs=[hbm] * 4 + [vmem],
        out_specs=(hbm,) * 4 + (vmem,),
        scratch_shapes=[
            pltpu.VMEM((parts, held, depth), bf16),
            pltpu.VMEM((parts, held, depth // 2), bf16),
            pltpu.VMEM((depth // 2, 2 * n * local), bf16),
            pltpu.VMEM((chunks, depth, width), bf16),
            pltpu.VMEM(scales.shape, f32),
            pltpu.VMEM(cotangent.shape, bf16),
            pltpu.VMEM(cotangent.shape, bf16),
        ]
        + [block] * 5
        + [
            pltpu.VMEM((2, 2, held, width), bf16),
            pltpu.VMEM((held, depth), f32),
            pltpu.VMEM((rows, width), f32),
            pltpu.VMEM((side, side), bf16),
            pltpu.VMEM((1, cols), f32),
            pltpu.VMEM((parts, held, depth), bf16),
            pltpu.VMEM((parts - 1, 2, held, piece), bf16),
            pltpu.VMEM((parts - 1, 2, held, piece), bf16),
            pltpu.VMEM((parts - 1, held, piece), bf16),
            pltpu.VMEM((parts - 1, held, piece), bf16),
            pltpu.VMEM((parts - 1, n, rows, piece), bf16),
            pltpu.VMEM((local, depth), bf16),
            pltpu.VMEM((2, rows, depth), bf16),
            pltpu.VMEM((2, rows, depth), bf16),
            pltpu.VMEM((rows, depth), bf16),
            dma((2,)),
            dma((chunks,)),
            dma((parts,)),
            dma((parts,)),
            dma,
            dma((2, 2)),
            dma,
        ]
        + [dma((parts, n))] * 2
        + [dma((parts,))] * 2
        + [dma((8,))]
        + [dma((n, items))]
        + [dma((items,))] * 4
        + [dma((2, parts))] * 2
        + [dma((2, parts - 1))] * 2,
        compiler_params=pltpu.CompilerParams(
            collective_id=0, has_side_effects=True, vmem_limit_bytes=63 * 1024 * 1024
        ),
        name="exchange",
    )(tokens, codes, scales, cotangent, sign_bits.reshape(cols // HB, HB))


def product_kernel(scaling, turned_ref, rotated_ref, act_ref, out_ref, act_out_ref):
    out_ref[...] = scaling * jnp.dot(turned_ref[...], rotated_ref[...], preferred_element_type=jnp.float32)
    act_out_ref[...] = act_ref[...]


def weight_product(turned, rotated, activation):
    rows, total = turned.shape
    width, local = rotated.shape[1], activation.shape[0]
    tile = next(t for t in (512, 256, HB) if width % t == 0)
    column = lambda c: (0, c)
    return pl.pallas_call(
        functools.partial(product_kernel, float(1.0 / (HB * total) ** 0.5)),
        grid=(width // tile,),
        out_shape=(
            jax.ShapeDtypeStruct((rows, width), jnp.float32),
            jax.ShapeDtypeStruct(activation.shape, activation.dtype),
        ),
        in_specs=[
            pl.BlockSpec((rows, total), lambda c: (0, 0)),
            pl.BlockSpec((total, tile), column),
            pl.BlockSpec((local, tile), column),
        ],
        out_specs=(pl.BlockSpec((rows, tile), column), pl.BlockSpec((local, tile), column)),
        compiler_params=pltpu.CompilerParams(vmem_limit_bytes=63 * 1024 * 1024),
        cost_estimate=pl.CostEstimate(
            flops=2 * rows * total * width, bytes_accessed=4 * rows * width + 2 * total * width, transcendentals=0
        ),
        name="weight_product",
    )(turned, rotated, activation)


def fits(tokens, codes, scales, cotangent, n_fsdp, n_tensor, parts, width):
    local, cols = cotangent.shape
    depth = codes.shape[0]
    if n_fsdp != 4 or n_tensor != 4 or lax.axis_size("replica") != 2:
        return False
    if local % (16 * parts) or cols % width or cols // width < 7 or depth % 1024 or (n_fsdp * local // parts) % HB:
        return False
    gathered = n_fsdp * local
    room = 2 * depth * cols + 10 * gathered * cols + 15 * gathered * depth + 4 * local * cols
    return room <= 56 * 1024 * 1024


def halve(array, keep, n_tensor, bit):
    lead = lax.dynamic_index_in_dim(array, keep, 0, keepdims=False)
    sent = lax.dynamic_index_in_dim(array, 1 - keep, 0, keepdims=False)
    came = lax.ppermute(sent, "tensor", [(t, t ^ bit) for t in range(n_tensor)])
    return (lead.astype(jnp.float32) + came.astype(jnp.float32)).astype(jnp.bfloat16)


def tensor_reduce(product, n_tensor):
    if n_tensor != 4:
        return lax.psum_scatter(product, "tensor", scatter_dimension=0, tiled=True)
    rows, cols = product.shape
    place = lax.axis_index("tensor")
    chunks = product.reshape(2, 2, rows // 4, cols).swapaxes(0, 1)
    chunks = halve(chunks, place % 2, n_tensor, 1)
    return halve(chunks, place // 2, n_tensor, 2)


def partner(array):
    return lax.ppermute(array, "replica", [(0, 1), (1, 0)])


def shards(tokens, weight_codes, scales, cotangent, sign_bits):
    n_fsdp, n_tensor = lax.axis_size("fsdp"), lax.axis_size("tensor")
    local_tokens = tokens.shape[0]
    shard_rows, hidden_cols = weight_codes.shape
    block_rows = shard_rows // scales.shape[0]
    swap = [(f * n_tensor + t, t * n_tensor + f) for f in range(n_fsdp) for t in range(n_tensor)]
    parts, width = 4, 512
    if fits(tokens, weight_codes, scales, cotangent, n_fsdp, n_tensor, parts, width):
        activation, turned, rotated, early, last = exchange(
            tokens, weight_codes, scales, cotangent, sign_bits, n_fsdp, parts, width
        )
        last = lax.ppermute(last, ("fsdp", "tensor"), swap)
        grad_codes, activation = weight_product(turned, rotated, activation)
        return (activation, jnp.concatenate([early, last], axis=0), grad_codes)
    weight = (
        (
            weight_codes.astype(jnp.float32).reshape(scales.shape[0], block_rows, hidden_cols)
            * scales[:, None, :]
        )
        .reshape(shard_rows, hidden_cols)
        .astype(jnp.bfloat16)
    )
    piece = shard_rows // n_tensor
    own = lax.dynamic_slice_in_dim(
        tokens.reshape(local_tokens, n_fsdp, shard_rows), lax.axis_index("tensor") * piece, piece, 2
    ).reshape(local_tokens, n_fsdp * piece)
    quarter = lax.all_to_all(own, "fsdp", split_axis=1, concat_axis=0, tiled=True)
    columns = lax.all_gather(quarter, "tensor", axis=1, tiled=True)
    half_rows = shard_rows // 2
    replica = lax.axis_index("replica")
    kept = lax.dynamic_slice_in_dim(columns, replica * half_rows, half_rows, 1)
    across = partner(lax.dynamic_slice_in_dim(columns, (1 - replica) * half_rows, half_rows, 1))
    hidden = lax.psum_scatter(
        jnp.dot(columns, weight, preferred_element_type=jnp.float32).astype(jnp.bfloat16),
        "fsdp",
        scatter_dimension=0,
        tiled=True,
    ).astype(jnp.float32)
    sigmoid_val = jax.nn.sigmoid(hidden)
    activation = (hidden * sigmoid_val).astype(jnp.bfloat16)
    hidden_grad = (
        cotangent.astype(jnp.float32) * sigmoid_val * (1.0 + hidden * (1.0 - sigmoid_val))
    ).astype(jnp.bfloat16)
    arrived = lax.all_gather(hidden_grad, "fsdp", axis=0, tiled=True)
    other = partner(arrived)
    product = lax.dot_general(
        arrived, weight, (((1,), (1,)), ((), ())), preferred_element_type=jnp.float32
    ).astype(jnp.bfloat16)
    turned = jnp.concatenate([kept, across], axis=0).T
    if n_fsdp == n_tensor:
        input_grad = lax.ppermute(tensor_reduce(product, n_tensor), ("fsdp", "tensor"), swap)
    else:
        returned = lax.all_to_all(product, "fsdp", split_axis=0, concat_axis=1, tiled=True)
        input_grad = lax.psum_scatter(returned, "tensor", scatter_dimension=1, tiled=True)
    grad_codes = rotated_grad(turned, arrived, other, sign_bits)
    return (activation, input_grad, grad_codes)


def solution(mesh):
    return jax.shard_map(
        shards,
        mesh=mesh,
        in_specs=(
            P(("fsdp", "replica"), None),
            P("fsdp", "tensor"),
            P("fsdp", "tensor"),
            P(("fsdp", "replica"), "tensor"),
            P("tensor"),
        ),
        out_specs=(
            P(("fsdp", "replica"), "tensor"),
            P(("fsdp", "replica"), "tensor"),
            P(("fsdp", "replica"), "tensor"),
        ),
        check_vma=False,
    )
```
